32 devices in a mesh: fsdp: 8 (over z, y), ctx: 4 (over x, core).
Axes of the slice: x: 2, y: 2, z: 4, core: 2. Of those that a mesh axis runs over, the one named last changes fastest.
Arguments:
- block_input: bfloat16 [8192, 1024], P(('fsdp', 'ctx')), may hold values from -6 to 6
- ln1_gain: bfloat16 [1024], P('fsdp'), may hold values from 0.5 to 1.5
- ln1_bias: bfloat16 [1024], P('fsdp'), may hold values from -1.5 to 1.5
- qkv_weight: bfloat16 [1024, 3, 1024], P('fsdp', None, 'ctx'), may hold values from -0.1875 to 0.1875
- qv_bias: bfloat16 [2, 1024], P(None, 'fsdp'), may hold values from -2.5 to 2.5
- out_weight: bfloat16 [1024, 1024], P(('ctx', 'fsdp')), may hold values from -1.5 to 1.5
- out_bias: bfloat16 [1024], P('fsdp'), may hold values from -1.5 to 1.5
- ln2_gain: bfloat16 [1024], P('fsdp'), may hold values from 0.5 to 1.5
- ln2_bias: bfloat16 [1024], P('fsdp'), may hold values from -1.5 to 1.5
- up_weight: bfloat16 [1024, 4096], P('fsdp', 'ctx'), may hold values from -0.1875 to 0.1875
- up_bias: bfloat16 [4096], P('fsdp'), may hold values from -2.5 to 2.5
- down_weight: bfloat16 [4096, 1024], P(('ctx', 'fsdp')), may hold values from -0.1875 to 0.1875
- down_bias: bfloat16 [1024], P('fsdp'), may hold values from -1.5 to 1.5
- doc_ids: int32 [8, 1024], P('fsdp'), may hold values from -1 to 7, as said below
- cotangent: bfloat16 [8192, 1024], P(('fsdp', 'ctx')), may hold values from -6 to 6
Outputs:
- output: bfloat16 [8192, 1024], P(('fsdp', 'ctx'))
- input_grad: float32 [8192, 1024], P(('fsdp', 'ctx'))
- ln1_gain_grad: float32 [1024], P('fsdp')
- ln1_bias_grad: float32 [1024], P('fsdp')
- qkv_weight_grad: float32 [1024, 3, 1024], P('fsdp', None, 'ctx')
- qv_bias_grad: float32 [2, 1024], P(None, 'fsdp')
- out_weight_grad: float32 [1024, 1024], P(('ctx', 'fsdp'))
- out_bias_grad: float32 [1024], P('fsdp')
- ln2_gain_grad: float32 [1024], P('fsdp')
- ln2_bias_grad: float32 [1024], P('fsdp')
- up_weight_grad: float32 [1024, 4096], P('fsdp', 'ctx')
- up_bias_grad: float32 [4096], P('fsdp')
- down_weight_grad: float32 [4096, 1024], P(('ctx', 'fsdp'))
- down_bias_grad: float32 [1024], P('fsdp')
The draws below stay inside these ranges and needn't reach their ends.
Inputs may be any that keep to these rules, and one draw needn't show every extreme that they name: `doc_ids`: along each group, numbers start at 0 and rise by one from one sequence to the next; padding (-1) only at a group's end. A sequence holds 128 to 1024 positions, except that a group's last sequence may be cut short; some sequence holds exactly 1024; some group has no padding and some group is half padding.
All inputs are finite; a program needn't handle non-finite values.
Results may differ from the reference program's by a relative error of at most 0.02.
Values may be sent and summed in bfloat16 or wider, within the bound.
A program may use at most 128 MiB of HBM per device.

```python
import jax
import jax.numpy as jnp
from jax import lax

D = 1024
HEADS = 16
HD = 64
FF = 4096
SEQ_MAX = 1024
CAP = 1024
TOKENS = 8192
QB = 512
SLOTS = 10
N_FSDP = 8


def draw_doc_ids(key, part):
    least = max(1, SEQ_MAX // 8)
    key_lengths, key_chosen, key_cuts = jax.random.split(key, 3)
    lengths = jax.random.randint(key_lengths, (N_FSDP, SLOTS), least, SEQ_MAX + 1, dtype=jnp.int32)
    chosen = jax.random.randint(key_chosen, (), 0, N_FSDP, dtype=jnp.int32)
    group_index = jnp.arange(N_FSDP, dtype=jnp.int32)
    column = jnp.arange(SLOTS, dtype=jnp.int32)
    shortest = (chosen + 2) % N_FSDP
    lengths = jnp.where((group_index == shortest)[:, None], least, lengths)
    first = (group_index[:, None] == chosen) & (column[None, :] == 0)
    lengths = jnp.where(first, SEQ_MAX, lengths)
    cuts = jax.random.randint(key_cuts, (N_FSDP,), 0, CAP // 2 + 1, dtype=jnp.int32)
    filled = CAP - cuts
    filled = jnp.where(group_index == chosen, CAP, filled)
    filled = jnp.where(group_index == (chosen + 1) % N_FSDP, CAP // 2, filled)
    filled = jnp.where(group_index == shortest, CAP, filled)
    ends = jnp.cumsum(lengths, axis=1)
    places = jnp.arange(CAP, dtype=jnp.int32)
    numbers = jnp.sum((places[None, :, None] >= ends[:, None, :]).astype(jnp.int32), axis=2)
    return jnp.where(places[None, :] < filled[:, None], numbers, -1).astype(jnp.int32)


def level_of(stream_key, extent, cuts, low, high):
    level, own = 1.0, jax.random.fold_in(stream_key, 6)
    for dim, parts in cuts:
        steps = jnp.exp(jax.random.uniform(jax.random.fold_in(own, dim), (parts,), jnp.float32, low / len(cuts), high / len(cuts)))
        level = level * jnp.repeat(steps, extent[dim] // parts).reshape([-1 if axis == dim else 1 for axis in range(len(extent))])
    return level


def bell_draw(rng, shape, deviation, most, cuts=(), held_as=jnp.bfloat16):
    drawn = deviation * jax.random.normal(rng, shape, jnp.float32)
    if cuts:
        drawn = drawn * level_of(rng, shape, cuts, -0.22, 0.18)
    return jnp.clip(drawn, -most, most).astype(held_as)


def setup_inputs(seed: int = 0) -> dict:
    streams_of = jax.random.split(jax.random.key(seed), 16)
    return {
        "block_input": bell_draw(streams_of[0], (TOKENS, D), 1.0, 6.0, ((0, 32),)),
        "ln1_gain": jnp.clip(1.0 + 0.1 * jax.random.normal(streams_of[1], (D,), jnp.float32), 0.5, 1.5).astype(jnp.bfloat16),
        "ln1_bias": bell_draw(streams_of[2], (D,), 0.3, 1.5, ((0, 8),)),
        "qkv_weight": bell_draw(streams_of[3], (D, 3, D), D ** -0.5, 0.1875, ((0, 8), (2, 4))),
        "qv_bias": bell_draw(streams_of[4], (2, D), 0.5, 2.5, ((1, 8),)),
        "out_weight": bell_draw(streams_of[5], (D, D), (D // 64) ** -0.5, 1.5, ((0, 32),)),
        "out_bias": bell_draw(streams_of[6], (D,), 0.3, 1.5, ((0, 8),)),
        "ln2_gain": jnp.clip(1.0 + 0.1 * jax.random.normal(streams_of[7], (D,), jnp.float32), 0.5, 1.5).astype(jnp.bfloat16),
        "ln2_bias": bell_draw(streams_of[8], (D,), 0.3, 1.5, ((0, 8),)),
        "up_weight": bell_draw(streams_of[9], (D, FF), D ** -0.5, 0.1875, ((0, 8), (1, 4))),
        "up_bias": bell_draw(streams_of[10], (FF,), 0.5, 2.5, ((0, 8),)),
        "down_weight": bell_draw(streams_of[11], (FF, D), (FF // 4) ** -0.5, 0.1875, ((0, 32),)),
        "down_bias": bell_draw(streams_of[12], (D,), 0.3, 1.5, ((0, 8),)),
        "doc_ids": draw_doc_ids(jax.random.fold_in(streams_of[15], 71), 0),
        "cotangent": bell_draw(streams_of[14], (TOKENS, D), 1.0, 6.0, ((0, 32),)),
    }


eps = 1e-05

@jax.custom_vjp
def low(v):
    return lax.optimization_barrier(v.astype(jnp.bfloat16)).astype(jnp.float32)

@jax.custom_vjp
def low_back(v):
    return v

def low_keep(v):
    return (low(v), None)

def low_pass(kept, grad):
    return (grad,)

def back_keep(v):
    return (v, None)

def back_low(kept, grad):
    return (low(grad),)
low.defvjp(low_keep, low_pass)
low_back.defvjp(back_keep, back_low)

def layer_norm(values, gain, shift):
    centre = values - lax.optimization_barrier(jnp.mean(values, axis=-1, keepdims=True))
    spread = lax.optimization_barrier(jnp.mean(centre * centre, axis=-1, keepdims=True))
    return centre * lax.rsqrt(spread + eps) * gain + shift

def gelu_tanh(values):
    return 0.5 * values * (1.0 + jnp.tanh(0.7978845608028654 * (values + 0.044715 * values * values * values)))

def matmul(left, right):
    return jnp.dot(left, right, precision=lax.Precision.HIGHEST, preferred_element_type=jnp.float32)

def forward_group(params, inputs, seq_ids):
    gain_one, shift_one, w_qkv, qv_shift, w_out, out_shift, gain_two, shift_two, w_up, up_shift, w_down, down_shift = params
    h_one = low(layer_norm(inputs, gain_one, shift_one))
    qkv_shift = jnp.concatenate([qv_shift[0], jnp.zeros((D,), jnp.float32), qv_shift[1]])
    qkv = low(low_back(matmul(h_one, w_qkv.reshape(D, 3 * D)) + qkv_shift))
    queries = qkv[:, :D].reshape(CAP, HEADS, HD)
    keys_all = qkv[:, D:2 * D].reshape(CAP, HEADS, HD)
    values_all = qkv[:, 2 * D:].reshape(CAP, HEADS, HD)
    places = jnp.arange(CAP, dtype=jnp.int32)
    factor = 1.0 / HD ** 0.5

    def one_block(start):
        query_blk = lax.dynamic_slice_in_dim(queries, start, QB, 0)
        ids_blk = lax.dynamic_slice_in_dim(seq_ids, start, QB, 0)
        rows_blk = start + jnp.arange(QB, dtype=jnp.int32)
        scores = jnp.einsum('qhd,khd->hqk', query_blk, keys_all, precision=lax.Precision.HIGHEST)
        scores = low_back(scores * factor)
        allowed = (ids_blk[:, None] == seq_ids[None, :]) & (places[None, :] <= rows_blk[:, None])
        scores = jnp.where(allowed[None], scores, -1000000000.0)
        top = lax.optimization_barrier(jnp.max(scores, axis=-1, keepdims=True))
        expo = jnp.exp(scores - top)
        probs = expo / lax.optimization_barrier(jnp.sum(expo, axis=-1, keepdims=True))
        return jnp.einsum('hqk,khd->qhd', low(probs), values_all, precision=lax.Precision.HIGHEST)
    starts = jnp.arange(CAP // QB, dtype=jnp.int32) * QB
    attended = lax.map(jax.checkpoint(one_block), starts).reshape(CAP, D)
    attended = low(low_back(attended))
    resid = inputs + low_back(matmul(attended, w_out) + out_shift)
    h_two = low(layer_norm(resid, gain_two, shift_two))
    pre_act = low_back(matmul(h_two, w_up) + up_shift)
    act_low = low(gelu_tanh(pre_act))
    return resid + low_back(matmul(act_low, w_down) + down_shift)

def reference(block_input, ln1_gain, ln1_bias, qkv_weight, qv_bias, out_weight, out_bias, ln2_gain, ln2_bias, up_weight, up_bias, down_weight, down_bias, doc_ids, cotangent):
    params = (ln1_gain.astype(jnp.float32), ln1_bias.astype(jnp.float32), qkv_weight.astype(jnp.float32), qv_bias.astype(jnp.float32), out_weight.astype(jnp.float32), out_bias.astype(jnp.float32), ln2_gain.astype(jnp.float32), ln2_bias.astype(jnp.float32), up_weight.astype(jnp.float32), up_bias.astype(jnp.float32), down_weight.astype(jnp.float32), down_bias.astype(jnp.float32))
    inputs_all = block_input.astype(jnp.float32).reshape(N_FSDP, CAP, D)
    live = (doc_ids >= 0).astype(jnp.float32)
    grads_in = cotangent.astype(jnp.float32).reshape(N_FSDP, CAP, D) * live[:, :, None]

    def step(totals, item):
        inputs, seq_ids, grad_in = item

        def apply_group(weights, values):
            return forward_group(weights, values, seq_ids)
        result, pull = jax.vjp(apply_group, params, inputs)
        grad_params, grad_inputs = pull(grad_in)
        summed = tuple((left + right for left, right in zip(totals, grad_params)))
        return (summed, (result.astype(jnp.bfloat16), grad_inputs))
    start_totals = tuple((jnp.zeros_like(weight) for weight in params))
    totals, (results, input_grads) = lax.scan(step, start_totals, (inputs_all, doc_ids, grads_in))
    return (results.reshape(TOKENS, D), input_grads.reshape(TOKENS, D), totals[0], totals[1], totals[2], totals[3], totals[4], totals[5], totals[6], totals[7], totals[8], totals[9], totals[10], totals[11])
```

```python
import jax
import jax.numpy as jnp
from jax import lax
from jax.sharding import PartitionSpec as P

HD = 64
FF = 4096


eps = 1e-05


def normalize(values):
    centre = values - jnp.mean(values, axis=-1, keepdims=True)
    spread = jnp.mean(centre * centre, axis=-1, keepdims=True)
    return centre * lax.rsqrt(spread + eps)


def gelu_tanh(values):
    return (
        0.5
        * values
        * (1.0 + jnp.tanh(0.7978845608028654 * (values + 0.044715 * values * values * values)))
    )


def contract_rows(left, right):
    return lax.dot_general(
        left, right, (((0,), (0,)), ((), ())), preferred_element_type=jnp.float32
    )


def contract_cols(left, right):
    return lax.dot_general(
        left, right, (((1,), (1,)), ((), ())), preferred_element_type=jnp.float32
    )


def split_fsdp():
    total = lax.axis_size("fsdp")
    inner = 2 if total <= 8 else 8
    return total // inner, inner


def move_fsdp(values, outer_step, inner_step):
    outer, inner = split_fsdp()
    pairs = [
        (a * inner + b, (a + outer_step) % outer * inner + (b + inner_step) % inner)
        for a in range(outer)
        for b in range(inner)
    ]
    return lax.ppermute(values, "fsdp", pairs)


def move_ctx(values, chip_step, core_step):
    chips = lax.axis_size("ctx") // 2
    pairs = [
        (x * 2 + c, (x + chip_step) % chips * 2 + (c + core_step) % 2)
        for x in range(chips)
        for c in range(2)
    ]
    return lax.ppermute(values, "ctx", pairs)


def put(buffer, values, place, axis):
    return lax.dynamic_update_index_in_dim(buffer, values, place, axis)


def pick(buffer, place, axis):
    return lax.dynamic_index_in_dim(buffer, place, axis, keepdims=False)


def gather_weight(shard):
    outer, inner = split_fsdp()
    place = lax.axis_index("fsdp")
    a, b = place // inner, place % inner
    held = put(jnp.zeros((outer,) + shard.shape, shard.dtype), shard, a, 0)
    for step in range(1, outer):
        held = put(held, move_fsdp(shard, step, 0), (a + outer - step) % outer, 0)
    if inner == 2:
        other = move_fsdp(held, 0, 1)
        first = b == 0
        whole = jnp.stack([jnp.where(first, held, other), jnp.where(first, other, held)], 1)
    else:
        whole = put(jnp.zeros((outer, inner) + shard.shape, shard.dtype), held, b, 1)
        for step in range(1, inner):
            whole = put(whole, move_fsdp(held, 0, step), (b + inner - step) % inner, 1)
    return whole.reshape((outer * inner,) + shard.shape)


def scatter_fsdp(parts, sent_type):
    outer, inner = split_fsdp()
    place = lax.axis_index("fsdp")
    a, b = place // inner, place % inner
    parts = parts.reshape((outer, inner) + parts.shape[1:])
    held = pick(parts, b, 1).astype(jnp.float32)
    for step in range(1, inner):
        sent = pick(parts, (b + step) % inner, 1).astype(sent_type)
        held = held + move_fsdp(sent, 0, step).astype(jnp.float32)
    summed = pick(held, a, 0)
    for step in range(1, outer):
        sent = pick(held, (a + step) % outer, 0).astype(sent_type)
        summed = summed + move_fsdp(sent, step, 0).astype(jnp.float32)
    return summed


def gather_rows(values):
    groups = lax.axis_size("ctx")
    chips = groups // 2
    place = lax.axis_index("ctx")
    x, core = place // 2, place % 2
    whole = jnp.zeros((groups,) + values.shape, values.dtype)
    for step in range(chips):
        got = values if step == 0 else move_ctx(values, step, 0)
        origin = (x + chips - step) % chips * 2
        whole = put(whole, got, origin + core, 0)
        whole = put(whole, move_ctx(got, 0, 1), origin + 1 - core, 0)
    return whole.reshape((groups * values.shape[0],) + values.shape[1:])


def reduce_rows(parts):
    groups = lax.axis_size("ctx")
    chips = groups // 2
    place = lax.axis_index("ctx")
    x, core = place // 2, place % 2
    parts = parts.reshape((chips, 2, parts.shape[0] // groups) + parts.shape[1:])
    sent = pick(parts, 1 - core, 1).astype(jnp.bfloat16)
    held = pick(parts, core, 1) + move_ctx(sent, 0, 1).astype(jnp.float32)
    summed = pick(held, x, 0)
    for step in range(1, chips):
        sent = pick(held, (x + step) % chips, 0).astype(jnp.bfloat16)
        summed = summed + move_ctx(sent, step, 0).astype(jnp.float32)
    return summed


def sum_ctx(values):
    chips = lax.axis_size("ctx") // 2
    total = values + move_ctx(values, 0, 1)
    whole = total
    for step in range(1, chips):
        whole = whole + move_ctx(total, step, 0)
    return whole


def project(inputs, weight):
    return jnp.dot(inputs, weight, preferred_element_type=jnp.float32)


def project_back(grad_low, weight):
    return contract_cols(grad_low, weight)


def weight_grad(inputs, grad_low):
    shards = lax.axis_size("fsdp")
    full = contract_rows(inputs, grad_low)
    return scatter_fsdp(
        full.reshape(shards, full.shape[0] // shards, full.shape[1]), jnp.bfloat16
    )


def block_scores(queries, keys_all, seq_ids, places, start, block, factor):
    query_blk = queries[start : start + block]
    scores = (
        jnp.einsum("qhd,khd->hqk", query_blk, keys_all, preferred_element_type=jnp.float32) * factor
    )
    allowed = (seq_ids[start : start + block, None] == seq_ids[None, :]) & (
        places[None, :] <= places[start : start + block, None]
    )
    return jnp.where(allowed[None], scores, -1000000000.0)


def attend(queries, keys_all, values_all, seq_ids, block, factor):
    places = jnp.arange(keys_all.shape[0], dtype=jnp.int32)
    outputs = []
    totals = []
    for start in range(0, keys_all.shape[0], block):
        scores = block_scores(queries, keys_all, seq_ids, places, start, block, factor)
        top = jnp.max(scores, axis=-1, keepdims=True)
        expo = jnp.exp(scores - top)
        summed = jnp.sum(expo, axis=-1, keepdims=True)
        probs_low = (expo / summed).astype(jnp.bfloat16)
        outputs.append(
            jnp.einsum("hqk,khd->qhd", probs_low, values_all, preferred_element_type=jnp.float32)
        )
        totals.append(top + jnp.log(summed))
    return (jnp.concatenate(outputs, 0), jnp.concatenate(totals, 1))


def attend_back(queries, keys_all, values_all, grad_heads, seq_ids, log_sums, block, factor):
    places = jnp.arange(keys_all.shape[0], dtype=jnp.int32)
    query_grads = []
    key_grad = jnp.zeros(keys_all.shape, jnp.float32)
    value_grad = jnp.zeros(values_all.shape, jnp.float32)
    for start in range(0, keys_all.shape[0], block):
        scores = block_scores(queries, keys_all, seq_ids, places, start, block, factor)
        probs = jnp.exp(scores - log_sums[:, start : start + block])
        grad_blk = grad_heads[start : start + block]
        grad_probs = jnp.einsum(
            "qhd,khd->hqk", grad_blk, values_all, preferred_element_type=jnp.float32
        )
        delta = jnp.sum(probs * grad_probs, axis=-1, keepdims=True)
        grad_scores = (probs * (grad_probs - delta)).astype(jnp.bfloat16)
        query_grads.append(
            jnp.einsum("hqk,khd->qhd", grad_scores, keys_all, preferred_element_type=jnp.float32)
            * factor
        )
        key_grad = (
            key_grad
            + jnp.einsum(
                "hqk,qhd->khd",
                grad_scores,
                queries[start : start + block],
                preferred_element_type=jnp.float32,
            )
            * factor
        )
        value_grad = value_grad + jnp.einsum(
            "hqk,qhd->khd", probs.astype(jnp.bfloat16), grad_blk, preferred_element_type=jnp.float32
        )
    return (jnp.concatenate(query_grads, 0), key_grad, value_grad)


def on_device(
    block_input,
    ln1_gain,
    ln1_bias,
    qkv_weight,
    qv_bias,
    out_weight,
    out_bias,
    ln2_gain,
    ln2_bias,
    up_weight,
    up_bias,
    down_weight,
    down_bias,
    doc_ids,
    cotangent,
):
    shards = lax.axis_size("fsdp")
    small = jnp.concatenate(
        [
            ln1_gain,
            ln1_bias,
            qv_bias[0],
            qv_bias[1],
            out_bias,
            ln2_gain,
            ln2_bias,
            down_bias,
            up_bias,
        ]
    )
    rows = block_input.shape[0]
    model = block_input.shape[1]
    groups = lax.axis_size("ctx")
    place = lax.axis_index("ctx")
    capacity = rows * groups
    width = qkv_weight.shape[2]
    heads_here = width // HD
    hidden_here = up_weight.shape[1]
    factor = 1.0 / HD**0.5
    block = min(512, capacity)
    group_ids = doc_ids[0]
    own_ids = lax.dynamic_slice_in_dim(group_ids, place * rows, rows)
    input_all = gather_rows(block_input)
    small_all = gather_weight(small.reshape(-1, 128)).reshape(shards, small.shape[0])
    piece = model // shards
    gain_one, shift_one, query_shift, value_shift, out_shift, gain_two, shift_two, down_shift = (
        small_all[:, i * piece : (i + 1) * piece].reshape(model) for i in range(8)
    )
    up_shift = small_all[:, 8 * piece :].reshape(-1)
    qv_full = jnp.stack([query_shift, value_shift])
    qkv_flat = gather_weight(qkv_weight.reshape(qkv_weight.shape[0], 3 * width)).reshape(
        model, 3 * width
    )
    out_full = gather_weight(out_weight).reshape(width, model)
    up_full = gather_weight(up_weight).reshape(model, hidden_here)
    down_full = gather_weight(down_weight).reshape(hidden_here, model)
    cot_all = gather_rows(cotangent)
    qv_here = lax.dynamic_slice_in_dim(qv_full.astype(jnp.float32), place * width, width, 1)
    qkv_shift = jnp.concatenate([qv_here[0], jnp.zeros((width,), jnp.float32), qv_here[1]])
    up_here = lax.dynamic_slice_in_dim(
        up_shift.astype(jnp.float32), place * hidden_here, hidden_here, 0
    )
    input_float = block_input.astype(jnp.float32)
    norm_one = normalize(input_float)
    h_one_all = (normalize(input_all.astype(jnp.float32)) * gain_one + shift_one).astype(
        jnp.bfloat16
    )
    qkv_proj = project(h_one_all, qkv_flat)
    qkv = (qkv_proj + qkv_shift).astype(jnp.bfloat16).reshape(capacity, 3, heads_here, HD)
    queries = qkv[:, 0]
    keys_all = qkv[:, 1]
    values_all = qkv[:, 2]
    attended, log_sums = attend(queries, keys_all, values_all, group_ids, block, factor)
    mixed_all = attended.astype(jnp.bfloat16).reshape(capacity, width)
    out_part = project(mixed_all, out_full)
    resid = input_float + reduce_rows(out_part) + out_shift
    norm_two = normalize(resid)
    h_two = (norm_two * gain_two + shift_two).astype(jnp.bfloat16)
    h_two_all = gather_rows(h_two)
    up_proj = project(h_two_all, up_full)
    pre_act = up_proj + up_here
    act, gelu_back = jax.vjp(gelu_tanh, pre_act)
    act_low = act.astype(jnp.bfloat16)
    down_part = project(act_low, down_full)
    output = (resid + reduce_rows(down_part) + down_shift).astype(jnp.bfloat16)
    live = (own_ids >= 0).astype(jnp.float32)
    grad_out = cotangent.astype(jnp.float32) * live[:, None]
    grad_low = grad_out.astype(jnp.bfloat16)
    down_shift_grad = jnp.sum(grad_low.astype(jnp.float32), axis=0)
    grad_all = jnp.where(group_ids[:, None] >= 0, cot_all, jnp.zeros_like(cot_all))
    down_grad = weight_grad(act_low, grad_all)
    grad_act = project_back(grad_all, down_full)
    grad_pre = gelu_back(grad_act)[0].astype(jnp.bfloat16)
    up_grad = weight_grad(h_two_all, grad_pre)
    up_sums = jnp.sum(grad_pre.astype(jnp.float32), axis=0)
    up_shift_grad = lax.dynamic_update_slice_in_dim(
        jnp.zeros((FF,), jnp.float32), up_sums, place * hidden_here, 0
    )
    grad_h_two = reduce_rows(project_back(grad_pre, up_full))
    gain_two_grad = jnp.sum(grad_h_two * norm_two, axis=0)
    shift_two_grad = jnp.sum(grad_h_two, axis=0)
    unused_two, norm_back_two = jax.vjp(normalize, resid)
    grad_resid = grad_out + norm_back_two(grad_h_two * gain_two.astype(jnp.float32))[0]
    resid_low = grad_resid.astype(jnp.bfloat16)
    out_shift_grad = jnp.sum(resid_low.astype(jnp.float32), axis=0)
    resid_all = gather_rows(resid_low)
    out_grad = weight_grad(mixed_all, resid_all)
    grad_heads = (
        project_back(resid_all, out_full).astype(jnp.bfloat16).reshape(capacity, heads_here, HD)
    )
    query_grad, key_grad, value_grad = attend_back(
        queries, keys_all, values_all, grad_heads, group_ids, log_sums, block, factor
    )
    grad_qkv = (
        jnp.stack([query_grad, key_grad, value_grad], 1)
        .astype(jnp.bfloat16)
        .reshape(capacity, 3 * width)
    )
    qkv_grad = weight_grad(h_one_all, grad_qkv).reshape(qkv_weight.shape[0], 3, width)
    column_sums = jnp.sum(grad_qkv.astype(jnp.float32), axis=0).reshape(3, width)
    qv_local = jnp.stack([column_sums[0], column_sums[2]])
    qv_grad = lax.dynamic_update_slice_in_dim(
        jnp.zeros((2, model), jnp.float32), qv_local, place * width, 1
    )
    grad_h_one = reduce_rows(project_back(grad_qkv, qkv_flat))
    gain_one_grad = jnp.sum(grad_h_one * norm_one, axis=0)
    shift_one_grad = jnp.sum(grad_h_one, axis=0)
    unused_one, norm_back_one = jax.vjp(normalize, input_float)
    input_grad = grad_resid + norm_back_one(grad_h_one * gain_one.astype(jnp.float32))[0]
    packed = jnp.concatenate(
        [
            part.reshape(shards, -1)
            for part in (
                gain_one_grad,
                shift_one_grad,
                qv_grad[0],
                qv_grad[1],
                out_shift_grad,
                gain_two_grad,
                shift_two_grad,
                down_shift_grad,
                up_shift_grad,
            )
        ],
        1,
    )
    sums = sum_ctx(scatter_fsdp(packed.reshape(shards, -1, 128), jnp.float32)).reshape(-1)
    (
        gain_one_sum,
        shift_one_sum,
        query_sum,
        value_sum,
        out_shift_sum,
        gain_two_sum,
        shift_two_sum,
        down_shift_sum,
    ) = (sums[i * piece : (i + 1) * piece] for i in range(8))
    qv_sum = jnp.stack([query_sum, value_sum])
    up_shift_sum = sums[8 * piece :]
    return (
        output,
        input_grad,
        gain_one_sum,
        shift_one_sum,
        qkv_grad,
        qv_sum,
        out_grad,
        out_shift_sum,
        gain_two_sum,
        shift_two_sum,
        up_grad,
        up_shift_sum,
        down_grad,
        down_shift_sum,
    )


def solution(mesh):
    placed = (
        P(("fsdp", "ctx"), None),
        P("fsdp"),
        P("fsdp"),
        P("fsdp", None, "ctx"),
        P(None, "fsdp"),
        P(("ctx", "fsdp"), None),
        P("fsdp"),
        P("fsdp"),
        P("fsdp"),
        P("fsdp", "ctx"),
        P("fsdp"),
        P(("ctx", "fsdp"), None),
        P("fsdp"),
        P("fsdp", None),
        P(("fsdp", "ctx"), None),
    )
    return jax.shard_map(
        on_device,
        mesh=mesh,
        in_specs=placed,
        out_specs=(
            P(("fsdp", "ctx"), None),
            P(("fsdp", "ctx"), None),
            P("fsdp"),
            P("fsdp"),
            P("fsdp", None, "ctx"),
            P(None, "fsdp"),
            P(("ctx", "fsdp"), None),
            P("fsdp"),
            P("fsdp"),
            P("fsdp"),
            P("fsdp", "ctx"),
            P("fsdp"),
            P(("ctx", "fsdp"), None),
            P("fsdp"),
        ),
        check_vma=False,
    )
```

```python
import functools

import jax
import jax.numpy as jnp
from jax import lax
from jax.experimental import pallas as pl
from jax.experimental.pallas import tpu as pltpu
from jax.sharding import PartitionSpec as P

HD = 64
FF = 4096


eps = 1e-05


def normalize(values):
    centre = values - jnp.mean(values, axis=-1, keepdims=True)
    spread = jnp.mean(centre * centre, axis=-1, keepdims=True)
    return centre * lax.rsqrt(spread + eps)


def gelu_tanh(values):
    return (
        0.5
        * values
        * (1.0 + jnp.tanh(0.7978845608028654 * (values + 0.044715 * values * values * values)))
    )


def contract_rows(left, right):
    return lax.dot_general(
        left, right, (((0,), (0,)), ((), ())), preferred_element_type=jnp.float32
    )


def contract_cols(left, right):
    return lax.dot_general(
        left, right, (((1,), (1,)), ((), ())), preferred_element_type=jnp.float32
    )


def split_fsdp():
    total = lax.axis_size("fsdp")
    inner = 2 if total <= 8 else 8
    return total // inner, inner


def move_fsdp(values, outer_step, inner_step):
    outer, inner = split_fsdp()
    pairs = [
        (a * inner + b, (a + outer_step) % outer * inner + (b + inner_step) % inner)
        for a in range(outer)
        for b in range(inner)
    ]
    return lax.ppermute(values, "fsdp", pairs)


def move_ctx(values, chip_step, core_step):
    chips = lax.axis_size("ctx") // 2
    pairs = [
        (x * 2 + c, (x + chip_step) % chips * 2 + (c + core_step) % 2)
        for x in range(chips)
        for c in range(2)
    ]
    return lax.ppermute(values, "ctx", pairs)


def put(buffer, values, place, axis):
    return lax.dynamic_update_index_in_dim(buffer, values, place, axis)


def pick(buffer, place, axis):
    return lax.dynamic_index_in_dim(buffer, place, axis, keepdims=False)


def gather_weight(shard):
    outer, inner = split_fsdp()
    place = lax.axis_index("fsdp")
    a, b = place // inner, place % inner
    held = put(jnp.zeros((outer,) + shard.shape, shard.dtype), shard, a, 0)
    for step in range(1, outer):
        held = put(held, move_fsdp(shard, step, 0), (a + outer - step) % outer, 0)
    if inner == 2:
        other = move_fsdp(held, 0, 1)
        first = b == 0
        whole = jnp.stack([jnp.where(first, held, other), jnp.where(first, other, held)], 1)
    else:
        whole = put(jnp.zeros((outer, inner) + shard.shape, shard.dtype), held, b, 1)
        for step in range(1, inner):
            whole = put(whole, move_fsdp(held, 0, step), (b + inner - step) % inner, 1)
    return whole.reshape((outer * inner,) + shard.shape)


def scatter_fsdp(parts, sent_type):
    outer, inner = split_fsdp()
    place = lax.axis_index("fsdp")
    a, b = place // inner, place % inner
    parts = parts.reshape((outer, inner) + parts.shape[1:])
    held = pick(parts, b, 1).astype(jnp.float32)
    for step in range(1, inner):
        sent = pick(parts, (b + step) % inner, 1).astype(sent_type)
        held = held + move_fsdp(sent, 0, step).astype(jnp.float32)
    summed = pick(held, a, 0)
    for step in range(1, outer):
        sent = pick(held, (a + step) % outer, 0).astype(sent_type)
        summed = summed + move_fsdp(sent, step, 0).astype(jnp.float32)
    return summed


def gather_rows(values):
    groups = lax.axis_size("ctx")
    chips = groups // 2
    place = lax.axis_index("ctx")
    x, core = place // 2, place % 2
    whole = jnp.zeros((groups,) + values.shape, values.dtype)
    for step in range(chips):
        got = values if step == 0 else move_ctx(values, step, 0)
        origin = (x + chips - step) % chips * 2
        whole = put(whole, got, origin + core, 0)
        whole = put(whole, move_ctx(got, 0, 1), origin + 1 - core, 0)
    return whole.reshape((groups * values.shape[0],) + values.shape[1:])


def reduce_rows(parts):
    groups = lax.axis_size("ctx")
    chips = groups // 2
    place = lax.axis_index("ctx")
    x, core = place // 2, place % 2
    parts = parts.reshape((chips, 2, parts.shape[0] // groups) + parts.shape[1:])
    sent = pick(parts, 1 - core, 1).astype(jnp.bfloat16)
    held = pick(parts, core, 1) + move_ctx(sent, 0, 1).astype(jnp.float32)
    summed = pick(held, x, 0)
    for step in range(1, chips):
        sent = pick(held, (x + step) % chips, 0).astype(jnp.bfloat16)
        summed = summed + move_ctx(sent, step, 0).astype(jnp.float32)
    return summed


def sum_ctx(values):
    chips = lax.axis_size("ctx") // 2
    total = values + move_ctx(values, 0, 1)
    whole = total
    for step in range(1, chips):
        whole = whole + move_ctx(total, step, 0)
    return whole


def project(inputs, weight):
    return jnp.dot(inputs, weight, preferred_element_type=jnp.float32)


def project_back(grad_low, weight):
    return contract_cols(grad_low, weight)


def weight_grad(inputs, grad_low):
    shards = lax.axis_size("fsdp")
    full = contract_rows(inputs, grad_low)
    return scatter_fsdp(
        full.reshape(shards, full.shape[0] // shards, full.shape[1]), jnp.bfloat16
    )


BLOCK = 256
MASKED = -1000000000.0


def masked_scores(queries, keys, ids_row_ref, ids_col_ref, start, stop):
    scores = contract_cols(keys, queries)
    same = ids_col_ref[:stop, :] == ids_row_ref[:, start:stop]
    key_place = lax.broadcasted_iota(jnp.int32, scores.shape, 0)
    query_place = lax.broadcasted_iota(jnp.int32, scores.shape, 1) + start
    return jnp.where(same & (key_place <= query_place), scores, MASKED)


def attend_kernel(heads, block, factor, qkv_ref, ids_row_ref, ids_col_ref, out_ref, lse_ref):
    rows = qkv_ref.shape[0]
    width = heads * HD
    for start in range(0, rows, block):
        stop = start + block
        for head in range(heads):
            lo, hi = head * HD, (head + 1) * HD
            queries = qkv_ref[start:stop, lo:hi] * jnp.asarray(factor, jnp.bfloat16)
            keys = qkv_ref[:stop, width + lo : width + hi]
            values = qkv_ref[:stop, 2 * width + lo : 2 * width + hi]
            scores = masked_scores(queries, keys, ids_row_ref, ids_col_ref, start, stop)
            top = jnp.max(scores, axis=0, keepdims=True)
            expo = jnp.exp(scores - top)
            summed = jnp.sum(expo, axis=0, keepdims=True)
            probs_low = (expo * (1.0 / summed)).astype(jnp.bfloat16)
            out_ref[start:stop, lo:hi] = contract_rows(values, probs_low).T.astype(jnp.bfloat16)
            lse_ref[head : head + 1, start:stop] = top + jnp.log(summed)


def attend_back_kernel(
    heads, block, factor, qkv_ref, grad_ref, lse_ref, ids_row_ref, ids_col_ref, out_ref, key_acc, value_acc
):
    rows = qkv_ref.shape[0]
    width = heads * HD
    for head in range(heads):
        lo, hi = head * HD, (head + 1) * HD
        for start in reversed(range(0, rows, block)):
            stop = start + block
            queries = qkv_ref[start:stop, lo:hi] * jnp.asarray(factor, jnp.bfloat16)
            keys = qkv_ref[:stop, width + lo : width + hi]
            values = qkv_ref[:stop, 2 * width + lo : 2 * width + hi]
            grads = grad_ref[start:stop, lo:hi]
            scores = masked_scores(queries, keys, ids_row_ref, ids_col_ref, start, stop)
            probs = jnp.exp(scores - lse_ref[head : head + 1, start:stop])
            grad_probs = contract_cols(values, grads)
            delta = jnp.sum(probs * grad_probs, axis=0, keepdims=True)
            grad_scores = (probs * (grad_probs - delta)).astype(jnp.bfloat16)
            query_grad = contract_rows(keys, grad_scores).T * factor
            out_ref[start:stop, lo:hi] = query_grad.astype(jnp.bfloat16)
            key_grad = jnp.dot(grad_scores, queries, preferred_element_type=jnp.float32)
            value_grad = jnp.dot(
                probs.astype(jnp.bfloat16), grads, preferred_element_type=jnp.float32
            )
            if stop == rows:
                key_acc[...] = key_grad
                value_acc[...] = value_grad
            else:
                key_acc[:stop, :] += key_grad
                value_acc[:stop, :] += value_grad
        out_ref[:, width + lo : width + hi] = key_acc[...].astype(jnp.bfloat16)
        out_ref[:, 2 * width + lo : 2 * width + hi] = value_acc[...].astype(jnp.bfloat16)


def attend(qkv, seq_ids, heads, factor):
    rows = qkv.shape[0]
    block = min(BLOCK, rows)
    return pl.pallas_call(
        functools.partial(attend_kernel, heads, block, factor),
        out_shape=(
            jax.ShapeDtypeStruct((rows, heads * HD), jnp.bfloat16),
            jax.ShapeDtypeStruct((heads, rows), jnp.float32),
        ),
        compiler_params=pltpu.CompilerParams(vmem_limit_bytes=40 * 2**20),
        cost_estimate=pl.CostEstimate(
            flops=4 * rows * rows * 256 * heads,
            bytes_accessed=8 * rows * heads * HD,
            transcendentals=rows * rows * heads,
        ),
        name="attend",
    )(qkv, seq_ids[None, :], seq_ids[:, None])


def attend_back(qkv, grads, log_sums, seq_ids, heads, factor):
    rows = qkv.shape[0]
    block = min(BLOCK, rows)
    return pl.pallas_call(
        functools.partial(attend_back_kernel, heads, block, factor),
        out_shape=jax.ShapeDtypeStruct(qkv.shape, jnp.bfloat16),
        scratch_shapes=[pltpu.VMEM((rows, HD), jnp.float32)] * 2,
        compiler_params=pltpu.CompilerParams(vmem_limit_bytes=40 * 2**20),
        cost_estimate=pl.CostEstimate(
            flops=10 * rows * rows * 256 * heads,
            bytes_accessed=14 * rows * heads * HD,
            transcendentals=rows * rows * heads,
        ),
        name="attend_back",
    )(qkv, grads, log_sums, seq_ids[None, :], seq_ids[:, None])


def on_device(
    block_input,
    ln1_gain,
    ln1_bias,
    qkv_weight,
    qv_bias,
    out_weight,
    out_bias,
    ln2_gain,
    ln2_bias,
    up_weight,
    up_bias,
    down_weight,
    down_bias,
    doc_ids,
    cotangent,
):
    shards = lax.axis_size("fsdp")
    small = jnp.concatenate(
        [
            ln1_gain,
            ln1_bias,
            qv_bias[0],
            qv_bias[1],
            out_bias,
            ln2_gain,
            ln2_bias,
            down_bias,
            up_bias,
        ]
    )
    rows = block_input.shape[0]
    model = block_input.shape[1]
    groups = lax.axis_size("ctx")
    place = lax.axis_index("ctx")
    capacity = rows * groups
    width = qkv_weight.shape[2]
    heads_here = width // HD
    hidden_here = up_weight.shape[1]
    factor = 1.0 / HD**0.5
    group_ids = doc_ids[0]
    own_ids = lax.dynamic_slice_in_dim(group_ids, place * rows, rows)
    input_all = gather_rows(block_input)
    qkv_rows = qkv_weight.shape[0]
    small_rows = -(-small.shape[0] // (3 * width * 16)) * 16
    first = jnp.concatenate(
        [
            qkv_weight.reshape(qkv_rows, 3 * width),
            jnp.pad(small, (0, small_rows * 3 * width - small.shape[0])).reshape(
                small_rows, 3 * width
            ),
        ]
    )
    first_all = gather_weight(first)
    small_all = first_all[:, qkv_rows:].reshape(shards, -1)[:, : small.shape[0]]
    piece = model // shards
    gain_one, shift_one, query_shift, value_shift, out_shift, gain_two, shift_two, down_shift = (
        small_all[:, i * piece : (i + 1) * piece].reshape(model) for i in range(8)
    )
    up_shift = small_all[:, 8 * piece :].reshape(-1)
    qv_full = jnp.stack([query_shift, value_shift])
    qkv_flat = first_all[:, :qkv_rows].reshape(model, 3 * width)
    out_full = gather_weight(out_weight).reshape(width, model)
    up_full = gather_weight(up_weight).reshape(model, hidden_here)
    down_full = gather_weight(down_weight).reshape(hidden_here, model)
    cot_all = gather_rows(cotangent)
    qv_here = lax.dynamic_slice_in_dim(qv_full.astype(jnp.float32), place * width, width, 1)
    qkv_shift = jnp.concatenate([qv_here[0], jnp.zeros((width,), jnp.float32), qv_here[1]])
    up_here = lax.dynamic_slice_in_dim(
        up_shift.astype(jnp.float32), place * hidden_here, hidden_here, 0
    )
    input_float = block_input.astype(jnp.float32)
    norm_one_all = normalize(input_all.astype(jnp.float32))
    h_one_all = (norm_one_all * gain_one + shift_one).astype(jnp.bfloat16)
    qkv_proj = project(h_one_all, qkv_flat)
    qkv = (qkv_proj + qkv_shift).astype(jnp.bfloat16)
    mixed_all, log_sums = attend(qkv, group_ids, heads_here, factor)
    out_part = project(mixed_all, out_full)
    resid = input_float + reduce_rows(out_part) + out_shift
    norm_two = normalize(resid)
    h_two = (norm_two * gain_two + shift_two).astype(jnp.bfloat16)
    h_two_all = gather_rows(h_two)
    up_proj = project(h_two_all, up_full)
    pre_act = up_proj + up_here
    act, gelu_back = jax.vjp(gelu_tanh, pre_act)
    act_low = act.astype(jnp.bfloat16)
    down_part = project(act_low, down_full)
    output = (resid + reduce_rows(down_part) + down_shift).astype(jnp.bfloat16)
    live = (own_ids >= 0).astype(jnp.float32)
    grad_out = cotangent.astype(jnp.float32) * live[:, None]
    grad_low = grad_out.astype(jnp.bfloat16)
    down_shift_grad = jnp.sum(grad_low.astype(jnp.float32), axis=0)
    grad_all = jnp.where(group_ids[:, None] >= 0, cot_all, jnp.zeros_like(cot_all))
    down_grad = weight_grad(act_low, grad_all)
    grad_act = project_back(grad_all, down_full)
    grad_pre = gelu_back(grad_act)[0].astype(jnp.bfloat16)
    up_grad = weight_grad(h_two_all, grad_pre)
    up_sums = jnp.sum(grad_pre.astype(jnp.float32), axis=0)
    up_shift_grad = lax.dynamic_update_slice_in_dim(
        jnp.zeros((FF,), jnp.float32), up_sums, place * hidden_here, 0
    )
    grad_h_two = reduce_rows(project_back(grad_pre, up_full))
    gain_two_grad = jnp.sum(grad_h_two * norm_two, axis=0)
    shift_two_grad = jnp.sum(grad_h_two, axis=0)
    unused_two, norm_back_two = jax.vjp(normalize, resid)
    grad_resid = grad_out + norm_back_two(grad_h_two * gain_two.astype(jnp.float32))[0]
    resid_low = grad_resid.astype(jnp.bfloat16)
    out_shift_grad = jnp.sum(resid_low.astype(jnp.float32), axis=0)
    resid_all = gather_rows(resid_low)
    out_grad = weight_grad(mixed_all, resid_all)
    grad_heads = project_back(resid_all, out_full).astype(jnp.bfloat16)
    grad_qkv = attend_back(qkv, grad_heads, log_sums, group_ids, heads_here, factor)
    qkv_grad = weight_grad(h_one_all, grad_qkv).reshape(qkv_weight.shape[0], 3, width)
    column_sums = jnp.sum(grad_qkv.astype(jnp.float32), axis=0).reshape(3, width)
    qv_local = jnp.stack([column_sums[0], column_sums[2]])
    qv_grad = lax.dynamic_update_slice_in_dim(
        jnp.zeros((2, model), jnp.float32), qv_local, place * width, 1
    )
    grad_h_one_part = project_back(grad_qkv, qkv_flat)
    gain_one_grad = jnp.sum(grad_h_one_part * norm_one_all, axis=0)
    shift_one_grad = jnp.sum(grad_h_one_part, axis=0)
    grad_h_one = reduce_rows(grad_h_one_part)
    unused_one, norm_back_one = jax.vjp(normalize, input_float)
    input_grad = grad_resid + norm_back_one(grad_h_one * gain_one.astype(jnp.float32))[0]
    packed = jnp.concatenate(
        [
            part.reshape(shards, -1)
            for part in (
                gain_one_grad,
                shift_one_grad,
                qv_grad[0],
                qv_grad[1],
                out_shift_grad,
                gain_two_grad,
                shift_two_grad,
                down_shift_grad,
                up_shift_grad,
            )
        ],
        1,
    )
    sums = sum_ctx(scatter_fsdp(packed.reshape(shards, -1, 128), jnp.float32)).reshape(-1)
    (
        gain_one_sum,
        shift_one_sum,
        query_sum,
        value_sum,
        out_shift_sum,
        gain_two_sum,
        shift_two_sum,
        down_shift_sum,
    ) = (sums[i * piece : (i + 1) * piece] for i in range(8))
    qv_sum = jnp.stack([query_sum, value_sum])
    up_shift_sum = sums[8 * piece :]
    return (
        output,
        input_grad,
        gain_one_sum,
        shift_one_sum,
        qkv_grad,
        qv_sum,
        out_grad,
        out_shift_sum,
        gain_two_sum,
        shift_two_sum,
        up_grad,
        up_shift_sum,
        down_grad,
        down_shift_sum,
    )


def solution(mesh):
    placed = (
        P(("fsdp", "ctx"), None),
        P("fsdp"),
        P("fsdp"),
        P("fsdp", None, "ctx"),
        P(None, "fsdp"),
        P(("ctx", "fsdp"), None),
        P("fsdp"),
        P("fsdp"),
        P("fsdp"),
        P("fsdp", "ctx"),
        P("fsdp"),
        P(("ctx", "fsdp"), None),
        P("fsdp"),
        P("fsdp", None),
        P(("fsdp", "ctx"), None),
    )
    return jax.shard_map(
        on_device,
        mesh=mesh,
        in_specs=placed,
        out_specs=(
            P(("fsdp", "ctx"), None),
            P(("fsdp", "ctx"), None),
            P("fsdp"),
            P("fsdp"),
            P("fsdp", None, "ctx"),
            P(None, "fsdp"),
            P(("ctx", "fsdp"), None),
            P("fsdp"),
            P("fsdp"),
            P("fsdp"),
            P("fsdp", "ctx"),
            P("fsdp"),
            P(("ctx", "fsdp"), None),
            P("fsdp"),
        ),
        check_vma=False,
    )
```

```python
import functools

import jax
import jax.numpy as jnp
from jax import lax
from jax.experimental import pallas as pl
from jax.experimental.pallas import tpu as pltpu
from jax.sharding import PartitionSpec as P

HD = 64
FF = 4096


eps = 1e-05


def normalize(values):
    centre = values - jnp.mean(values, axis=-1, keepdims=True)
    spread = jnp.mean(centre * centre, axis=-1, keepdims=True)
    return centre * lax.rsqrt(spread + eps)


def contract_rows(left, right):
    return lax.dot_general(
        left, right, (((0,), (0,)), ((), ())), preferred_element_type=jnp.float32
    )


def contract_cols(left, right):
    return lax.dot_general(
        left, right, (((1,), (1,)), ((), ())), preferred_element_type=jnp.float32
    )


def split_fsdp():
    total = lax.axis_size("fsdp")
    inner = 2 if total <= 8 else 8
    return total // inner, inner


def move_fsdp(values, outer_step, inner_step):
    outer, inner = split_fsdp()
    pairs = [
        (a * inner + b, (a + outer_step) % outer * inner + (b + inner_step) % inner)
        for a in range(outer)
        for b in range(inner)
    ]
    return lax.ppermute(values, "fsdp", pairs)


def move_ctx(values, chip_step, core_step):
    chips = lax.axis_size("ctx") // 2
    pairs = [
        (x * 2 + c, (x + chip_step) % chips * 2 + (c + core_step) % 2)
        for x in range(chips)
        for c in range(2)
    ]
    return lax.ppermute(values, "ctx", pairs)


def put(buffer, values, place, axis):
    return lax.dynamic_update_index_in_dim(buffer, values, place, axis)


def pick(buffer, place, axis):
    return lax.dynamic_index_in_dim(buffer, place, axis, keepdims=False)


def gather_weight(shard):
    outer, inner = split_fsdp()
    place = lax.axis_index("fsdp")
    a, b = place // inner, place % inner
    held = put(jnp.zeros((outer,) + shard.shape, shard.dtype), shard, a, 0)
    for step in range(1, outer):
        held = put(held, move_fsdp(shard, step, 0), (a + outer - step) % outer, 0)
    if inner == 2:
        other = move_fsdp(held, 0, 1)
        first = b == 0
        whole = jnp.stack([jnp.where(first, held, other), jnp.where(first, other, held)], 1)
    else:
        whole = put(jnp.zeros((outer, inner) + shard.shape, shard.dtype), held, b, 1)
        for step in range(1, inner):
            whole = put(whole, move_fsdp(held, 0, step), (b + inner - step) % inner, 1)
    return whole.reshape((outer * inner,) + shard.shape)


def scatter_fsdp(parts, sent_type):
    outer, inner = split_fsdp()
    place = lax.axis_index("fsdp")
    a, b = place // inner, place % inner
    parts = parts.reshape((outer, inner) + parts.shape[1:])
    held = pick(parts, b, 1).astype(jnp.float32)
    for step in range(1, inner):
        sent = pick(parts, (b + step) % inner, 1).astype(sent_type)
        held = held + move_fsdp(sent, 0, step).astype(jnp.float32)
    summed = pick(held, a, 0)
    for step in range(1, outer):
        sent = pick(held, (a + step) % outer, 0).astype(sent_type)
        summed = summed + move_fsdp(sent, step, 0).astype(jnp.float32)
    return summed


def gather_rows(values):
    groups = lax.axis_size("ctx")
    chips = groups // 2
    place = lax.axis_index("ctx")
    x, core = place // 2, place % 2
    whole = jnp.zeros((groups,) + values.shape, values.dtype)
    for step in range(chips):
        got = values if step == 0 else move_ctx(values, step, 0)
        origin = (x + chips - step) % chips * 2
        whole = put(whole, got, origin + core, 0)
        whole = put(whole, move_ctx(got, 0, 1), origin + 1 - core, 0)
    return whole.reshape((groups * values.shape[0],) + values.shape[1:])


def reduce_rows(parts):
    groups = lax.axis_size("ctx")
    chips = groups // 2
    place = lax.axis_index("ctx")
    x, core = place // 2, place % 2
    parts = parts.reshape((chips, 2, parts.shape[0] // groups) + parts.shape[1:])
    sent = pick(parts, 1 - core, 1).astype(jnp.bfloat16)
    held = pick(parts, core, 1).astype(jnp.float32) + move_ctx(sent, 0, 1).astype(jnp.float32)
    summed = pick(held, x, 0)
    for step in range(1, chips):
        sent = pick(held, (x + step) % chips, 0).astype(jnp.bfloat16)
        summed = summed + move_ctx(sent, step, 0).astype(jnp.float32)
    return summed


def sum_ctx(values):
    chips = lax.axis_size("ctx") // 2
    total = values + move_ctx(values, 0, 1)
    whole = total
    for step in range(1, chips):
        whole = whole + move_ctx(total, step, 0)
    return whole


def project(inputs, weight):
    return jnp.dot(inputs, weight, preferred_element_type=jnp.float32)


def project_back(grad_low, weight):
    return contract_cols(grad_low, weight)


def weight_grad(inputs, grad_low):
    shards = lax.axis_size("fsdp")
    full = contract_rows(inputs, grad_low)
    return scatter_fsdp(
        full.reshape(shards, full.shape[0] // shards, full.shape[1]), jnp.bfloat16
    )


BLOCK = 256
MASKED = -1000000000.0


def masked_scores(queries, keys, ids_row_ref, ids_col_ref, start, stop):
    scores = contract_cols(keys, queries)
    same = ids_col_ref[:stop, :] == ids_row_ref[:, start:stop]
    key_place = lax.broadcasted_iota(jnp.int32, scores.shape, 0)
    query_place = lax.broadcasted_iota(jnp.int32, scores.shape, 1) + start
    return jnp.where(same & (key_place <= query_place), scores, MASKED)


def attend_kernel(heads, block, factor, qkv_ref, ids_row_ref, ids_col_ref, out_ref, lse_ref):
    rows = qkv_ref.shape[0]
    width = heads * HD
    for start in range(0, rows, block):
        stop = start + block
        for head in range(heads):
            lo, hi = head * HD, (head + 1) * HD
            queries = qkv_ref[start:stop, lo:hi] * jnp.asarray(factor, jnp.bfloat16)
            keys = qkv_ref[:stop, width + lo : width + hi]
            values = qkv_ref[:stop, 2 * width + lo : 2 * width + hi]
            scores = masked_scores(queries, keys, ids_row_ref, ids_col_ref, start, stop)
            top = jnp.max(scores, axis=0, keepdims=True)
            expo = jnp.exp(scores - top)
            summed = jnp.sum(expo, axis=0, keepdims=True)
            probs_low = (expo * (1.0 / summed)).astype(jnp.bfloat16)
            out_ref[start:stop, lo:hi] = contract_rows(values, probs_low).T.astype(jnp.bfloat16)
            lse_ref[head : head + 1, start:stop] = top + jnp.log(summed)


def attend_back_kernel(
    heads, block, factor, qkv_ref, grad_ref, lse_ref, ids_row_ref, ids_col_ref, out_ref, key_acc, value_acc
):
    rows = qkv_ref.shape[0]
    width = heads * HD
    for head in range(heads):
        lo, hi = head * HD, (head + 1) * HD
        for start in reversed(range(0, rows, block)):
            stop = start + block
            queries = qkv_ref[start:stop, lo:hi] * jnp.asarray(factor, jnp.bfloat16)
            keys = qkv_ref[:stop, width + lo : width + hi]
            values = qkv_ref[:stop, 2 * width + lo : 2 * width + hi]
            grads = grad_ref[start:stop, lo:hi]
            scores = masked_scores(queries, keys, ids_row_ref, ids_col_ref, start, stop)
            probs = jnp.exp(scores - lse_ref[head : head + 1, start:stop])
            grad_probs = contract_cols(values, grads)
            delta = jnp.sum(probs * grad_probs, axis=0, keepdims=True)
            grad_scores = (probs * (grad_probs - delta)).astype(jnp.bfloat16)
            query_grad = contract_rows(keys, grad_scores).T * factor
            out_ref[start:stop, lo:hi] = query_grad.astype(jnp.bfloat16)
            key_grad = jnp.dot(grad_scores, queries, preferred_element_type=jnp.float32)
            value_grad = jnp.dot(
                probs.astype(jnp.bfloat16), grads, preferred_element_type=jnp.float32
            )
            if stop == rows:
                key_acc[...] = key_grad
                value_acc[...] = value_grad
            else:
                key_acc[:stop, :] += key_grad
                value_acc[:stop, :] += value_grad
        out_ref[:, width + lo : width + hi] = key_acc[...].astype(jnp.bfloat16)
        out_ref[:, 2 * width + lo : 2 * width + hi] = value_acc[...].astype(jnp.bfloat16)


def attend(qkv, seq_ids, heads, factor):
    rows = qkv.shape[0]
    block = min(BLOCK, rows)
    return pl.pallas_call(
        functools.partial(attend_kernel, heads, block, factor),
        out_shape=(
            jax.ShapeDtypeStruct((rows, heads * HD), jnp.bfloat16),
            jax.ShapeDtypeStruct((heads, rows), jnp.float32),
        ),
        compiler_params=pltpu.CompilerParams(vmem_limit_bytes=40 * 2**20),
        cost_estimate=pl.CostEstimate(
            flops=4 * rows * rows * 256 * heads,
            bytes_accessed=8 * rows * heads * HD,
            transcendentals=rows * rows * heads,
        ),
        name="attend",
    )(qkv, seq_ids[None, :], seq_ids[:, None])


def attend_back(qkv, grads, log_sums, seq_ids, heads, factor):
    rows = qkv.shape[0]
    block = min(BLOCK, rows)
    return pl.pallas_call(
        functools.partial(attend_back_kernel, heads, block, factor),
        out_shape=jax.ShapeDtypeStruct(qkv.shape, jnp.bfloat16),
        scratch_shapes=[pltpu.VMEM((rows, HD), jnp.float32)] * 2,
        compiler_params=pltpu.CompilerParams(vmem_limit_bytes=40 * 2**20),
        cost_estimate=pl.CostEstimate(
            flops=10 * rows * rows * 256 * heads,
            bytes_accessed=14 * rows * heads * HD,
            transcendentals=rows * rows * heads,
        ),
        name="attend_back",
    )(qkv, grads, log_sums, seq_ids[None, :], seq_ids[:, None])


def mlp_kernel(
    in_ref,
    grad_ref,
    up_ref,
    shift_ref,
    down_ref,
    act_ref,
    pre_ref,
    sums_ref,
    out_ref,
    back_ref,
    out_acc,
    back_acc,
):
    step = pl.program_id(0)
    u = jnp.dot(in_ref[...], up_ref[...], preferred_element_type=jnp.float32) + shift_ref[...]
    square = u * u
    bent = jnp.tanh(0.7978845608028654 * (u * (1.0 + 0.044715 * square)))
    half = 0.5 * (1.0 + bent)
    act = (u * half).astype(jnp.bfloat16)
    act_ref[...] = act
    slope = half + 0.5 * u * (1.0 - bent * bent) * (
        0.7978845608028654 * (1.0 + 0.134145 * square)
    )
    grad_pre = (contract_cols(grad_ref[...], down_ref[...]) * slope).astype(jnp.bfloat16)
    pre_ref[...] = grad_pre
    sums_ref[...] = jnp.sum(grad_pre.astype(jnp.float32), axis=0, keepdims=True)
    out_part = jnp.dot(act, down_ref[...], preferred_element_type=jnp.float32)
    back_part = contract_cols(grad_pre, up_ref[...])

    @pl.when(step == 0)
    def _():
        out_acc[...] = out_part
        back_acc[...] = back_part

    @pl.when(step > 0)
    def _():
        out_acc[...] += out_part
        back_acc[...] += back_part

    @pl.when(step == pl.num_programs(0) - 1)
    def _():
        out_ref[...] = out_acc[...].astype(jnp.bfloat16)
        back_ref[...] = back_acc[...].astype(jnp.bfloat16)


def mlp(inputs, grads, up, shift, down):
    rows, model = inputs.shape
    hidden = up.shape[1]
    block = min(256, hidden)
    whole = pl.BlockSpec((rows, model), lambda i: (0, 0))
    columns = pl.BlockSpec((rows, block), lambda i: (0, i))
    line = pl.BlockSpec((1, block), lambda i: (0, i))
    return pl.pallas_call(
        mlp_kernel,
        grid=(hidden // block,),
        in_specs=[
            whole,
            whole,
            pl.BlockSpec((model, block), lambda i: (0, i)),
            line,
            pl.BlockSpec((block, model), lambda i: (i, 0)),
        ],
        out_specs=(columns, columns, line, whole, whole),
        out_shape=(
            jax.ShapeDtypeStruct((rows, hidden), jnp.bfloat16),
            jax.ShapeDtypeStruct((rows, hidden), jnp.bfloat16),
            jax.ShapeDtypeStruct((1, hidden), jnp.float32),
            jax.ShapeDtypeStruct((rows, model), jnp.bfloat16),
            jax.ShapeDtypeStruct((rows, model), jnp.bfloat16),
        ),
        scratch_shapes=[pltpu.VMEM((rows, model), jnp.float32)] * 2,
        compiler_params=pltpu.CompilerParams(vmem_limit_bytes=52 * 2**20),
        cost_estimate=pl.CostEstimate(
            flops=8 * rows * model * hidden,
            bytes_accessed=8 * rows * model + 4 * rows * hidden + 4 * model * hidden,
            transcendentals=rows * hidden,
        ),
        name="mlp",
    )(inputs, grads, up, shift[None, :], down)


def on_device(
    block_input,
    ln1_gain,
    ln1_bias,
    qkv_weight,
    qv_bias,
    out_weight,
    out_bias,
    ln2_gain,
    ln2_bias,
    up_weight,
    up_bias,
    down_weight,
    down_bias,
    doc_ids,
    cotangent,
):
    shards = lax.axis_size("fsdp")
    small = jnp.concatenate(
        [
            ln1_gain,
            ln1_bias,
            qv_bias[0],
            qv_bias[1],
            out_bias,
            ln2_gain,
            ln2_bias,
            down_bias,
            up_bias,
        ]
    )
    rows = block_input.shape[0]
    model = block_input.shape[1]
    groups = lax.axis_size("ctx")
    place = lax.axis_index("ctx")
    capacity = rows * groups
    width = qkv_weight.shape[2]
    heads_here = width // HD
    hidden_here = up_weight.shape[1]
    factor = 1.0 / HD**0.5
    group_ids = doc_ids[0]
    own_ids = lax.dynamic_slice_in_dim(group_ids, place * rows, rows)
    input_all = gather_rows(block_input)
    qkv_rows = qkv_weight.shape[0]
    small_rows = -(-small.shape[0] // (3 * width * 16)) * 16
    first = jnp.concatenate(
        [
            qkv_weight.reshape(qkv_rows, 3 * width),
            jnp.pad(small, (0, small_rows * 3 * width - small.shape[0])).reshape(
                small_rows, 3 * width
            ),
        ]
    )
    first_all = gather_weight(first)
    small_all = first_all[:, qkv_rows:].reshape(shards, -1)[:, : small.shape[0]]
    piece = model // shards
    gain_one, shift_one, query_shift, value_shift, out_shift, gain_two, shift_two, down_shift = (
        small_all[:, i * piece : (i + 1) * piece].reshape(model) for i in range(8)
    )
    up_shift = small_all[:, 8 * piece :].reshape(-1)
    qv_full = jnp.stack([query_shift, value_shift])
    qkv_flat = first_all[:, :qkv_rows].reshape(model, 3 * width)
    out_full = gather_weight(out_weight).reshape(width, model)
    up_full = gather_weight(up_weight).reshape(model, hidden_here)
    down_full = gather_weight(down_weight).reshape(hidden_here, model)
    cot_all = gather_rows(cotangent)
    qv_here = lax.dynamic_slice_in_dim(qv_full.astype(jnp.float32), place * width, width, 1)
    qkv_shift = jnp.concatenate([qv_here[0], jnp.zeros((width,), jnp.float32), qv_here[1]])
    up_here = lax.dynamic_slice_in_dim(
        up_shift.astype(jnp.float32), place * hidden_here, hidden_here, 0
    )
    input_float = block_input.astype(jnp.float32)
    norm_one_all = normalize(input_all.astype(jnp.float32))
    h_one_all = (norm_one_all * gain_one + shift_one).astype(jnp.bfloat16)
    qkv_proj = project(h_one_all, qkv_flat)
    qkv = (qkv_proj + qkv_shift).astype(jnp.bfloat16)
    mixed_all, log_sums = attend(qkv, group_ids, heads_here, factor)
    out_part = project(mixed_all, out_full)
    resid = input_float + reduce_rows(out_part) + out_shift
    norm_two = normalize(resid)
    h_two = (norm_two * gain_two + shift_two).astype(jnp.bfloat16)
    h_two_all = gather_rows(h_two)
    live = (own_ids >= 0).astype(jnp.float32)
    grad_out = cotangent.astype(jnp.float32) * live[:, None]
    grad_low = grad_out.astype(jnp.bfloat16)
    down_shift_grad = jnp.sum(grad_low.astype(jnp.float32), axis=0)
    grad_all = jnp.where(group_ids[:, None] >= 0, cot_all, jnp.zeros_like(cot_all))
    act_low, grad_pre, up_sums, down_part, back_part = mlp(
        h_two_all, grad_all, up_full, up_here, down_full
    )
    grad_h_two = reduce_rows(back_part)
    output = (resid + reduce_rows(down_part) + down_shift).astype(jnp.bfloat16)
    down_grad = weight_grad(act_low, grad_all)
    up_grad = weight_grad(h_two_all, grad_pre)
    up_sums = up_sums[0]
    up_shift_grad = lax.dynamic_update_slice_in_dim(
        jnp.zeros((FF,), jnp.float32), up_sums, place * hidden_here, 0
    )
    gain_two_grad = jnp.sum(grad_h_two * norm_two, axis=0)
    shift_two_grad = jnp.sum(grad_h_two, axis=0)
    unused_two, norm_back_two = jax.vjp(normalize, resid)
    grad_resid = grad_out + norm_back_two(grad_h_two * gain_two.astype(jnp.float32))[0]
    resid_low = grad_resid.astype(jnp.bfloat16)
    out_shift_grad = jnp.sum(resid_low.astype(jnp.float32), axis=0)
    resid_all = gather_rows(resid_low)
    out_grad = weight_grad(mixed_all, resid_all)
    grad_heads = project_back(resid_all, out_full).astype(jnp.bfloat16)
    grad_qkv = attend_back(qkv, grad_heads, log_sums, group_ids, heads_here, factor)
    qkv_grad = weight_grad(h_one_all, grad_qkv).reshape(qkv_weight.shape[0], 3, width)
    column_sums = jnp.sum(grad_qkv.astype(jnp.float32), axis=0).reshape(3, width)
    qv_local = jnp.stack([column_sums[0], column_sums[2]])
    qv_grad = lax.dynamic_update_slice_in_dim(
        jnp.zeros((2, model), jnp.float32), qv_local, place * width, 1
    )
    grad_h_one_part = project_back(grad_qkv, qkv_flat)
    gain_one_grad = jnp.sum(grad_h_one_part * norm_one_all, axis=0)
    shift_one_grad = jnp.sum(grad_h_one_part, axis=0)
    grad_h_one = reduce_rows(grad_h_one_part)
    unused_one, norm_back_one = jax.vjp(normalize, input_float)
    input_grad = grad_resid + norm_back_one(grad_h_one * gain_one.astype(jnp.float32))[0]
    packed = jnp.concatenate(
        [
            part.reshape(shards, -1)
            for part in (
                gain_one_grad,
                shift_one_grad,
                qv_grad[0],
                qv_grad[1],
                out_shift_grad,
                gain_two_grad,
                shift_two_grad,
                down_shift_grad,
                up_shift_grad,
            )
        ],
        1,
    )
    sums = sum_ctx(scatter_fsdp(packed.reshape(shards, -1, 128), jnp.float32)).reshape(-1)
    (
        gain_one_sum,
        shift_one_sum,
        query_sum,
        value_sum,
        out_shift_sum,
        gain_two_sum,
        shift_two_sum,
        down_shift_sum,
    ) = (sums[i * piece : (i + 1) * piece] for i in range(8))
    qv_sum = jnp.stack([query_sum, value_sum])
    up_shift_sum = sums[8 * piece :]
    return (
        output,
        input_grad,
        gain_one_sum,
        shift_one_sum,
        qkv_grad,
        qv_sum,
        out_grad,
        out_shift_sum,
        gain_two_sum,
        shift_two_sum,
        up_grad,
        up_shift_sum,
        down_grad,
        down_shift_sum,
    )


def solution(mesh):
    placed = (
        P(("fsdp", "ctx"), None),
        P("fsdp"),
        P("fsdp"),
        P("fsdp", None, "ctx"),
        P(None, "fsdp"),
        P(("ctx", "fsdp"), None),
        P("fsdp"),
        P("fsdp"),
        P("fsdp"),
        P("fsdp", "ctx"),
        P("fsdp"),
        P(("ctx", "fsdp"), None),
        P("fsdp"),
        P("fsdp", None),
        P(("fsdp", "ctx"), None),
    )
    return jax.shard_map(
        on_device,
        mesh=mesh,
        in_specs=placed,
        out_specs=(
            P(("fsdp", "ctx"), None),
            P(("fsdp", "ctx"), None),
            P("fsdp"),
            P("fsdp"),
            P("fsdp", None, "ctx"),
            P(None, "fsdp"),
            P(("ctx", "fsdp"), None),
            P("fsdp"),
            P("fsdp"),
            P("fsdp"),
            P("fsdp", "ctx"),
            P("fsdp"),
            P(("ctx", "fsdp"), None),
            P("fsdp"),
        ),
        check_vma=False,
    )
```
